512 devices in a mesh: row: 16 (over y_lo, x, core), col: 32 (over z, y_hi).
Axes of the slice: x: 4, y: 4 (y_hi: 2, y_lo: 2; y = y_hi * 2 + y_lo), z: 16, core: 2. Of those that a mesh axis runs over, the one named last changes fastest.
Arguments:
- coefficients: float32 [8, 8192, 8192], P(None, 'row', 'col'), may hold values from -40 to 40, as said below
- lambdas: float32 [256], replicated, may hold values from -0.95 to 0.95
- right_vecs: float32 [8192, 256], P(('col', 'row')), may hold values from -6 to 6
- left_vecs: float32 [8192, 256], P(('row', 'col')), may hold values from -6 to 6
Outputs:
- right_resid: float32 [8192, 256], P(('row', 'col'))
- left_resid: float32 [8192, 256], P(('col', 'row'))
- root_mean: float32 [2, 256], replicated
The draws below stay inside these ranges and needn't reach their ends.
Inputs may be any that keep to these rules, and one draw needn't show every extreme that they name: `coefficients`: the entries of every coefficient matrix.
All inputs are finite; a program needn't handle non-finite values.
Results may differ from the reference program's by a relative error of at most 0.0001.
Values sent between devices are 32-bit elements; how exact they have to be, the bound alone decides.
A program may use at most 64 MiB of HBM per device.

```python
import math
import jax
import jax.numpy as jnp
from jax import lax

N = 8192
K = 8
TRIP = 256


def draw_coefficients(key, part):
    subkeys = jax.random.split(jax.random.fold_in(key, 17), 3)
    positions = jnp.arange(N, dtype=jnp.float32) / N
    trend_scale = 3.0 ** (positions - 0.5)
    low_log = -0.5 * math.log(10.0)
    high_log = 0.5 * math.log(10.0)
    row_scale = trend_scale * jnp.exp(jax.random.uniform(subkeys[0], (N,), jnp.float32, low_log, high_log))
    col_scale = trend_scale * jnp.exp(jax.random.uniform(subkeys[1], (N,), jnp.float32, low_log, high_log))
    random_part = jnp.clip(jax.random.normal(subkeys[2], (K, N, N), jnp.float32), -6.0, 6.0)
    matrices = random_part / math.sqrt(N) * row_scale[None, :, None] * col_scale[None, None, :]
    identity_mask = (jnp.arange(N)[:, None] == jnp.arange(N)[None, :]).astype(jnp.float32)
    matrices = matrices.at[0].add(0.5 * identity_mask * (row_scale * col_scale)[:, None])
    return matrices


def levels(rng, dims, pieces, low, largest):
    def one(axis_at, parts):
        steps = jax.random.uniform(jax.random.fold_in(jax.random.fold_in(rng, 6), axis_at), (parts,), jnp.float32, low / len(pieces), largest / len(pieces))
        return jnp.repeat(jnp.exp(steps), dims[axis_at] // parts).reshape((-1,) + (1,) * (len(dims) - axis_at - 1))

    level = one(*pieces[0])
    for cut in pieces[1:]:
        level = level * one(*cut)
    return level


def scatter_about(stream_key, extent, scale, most, cuts=(), held_as=jnp.bfloat16):
    array = jax.random.normal(stream_key, extent, jnp.float32) * scale
    if len(cuts) > 0:
        array = levels(stream_key, extent, cuts, -0.22, 0.18) * array
    return jnp.clip(array, min=-most, max=most).astype(held_as)


def setup_inputs(seed: int = 0) -> dict:
    splits = jax.random.split(jax.random.key(seed), 5)
    coefficients = draw_coefficients(jax.random.fold_in(splits[4], 71), 0)
    lambdas = jnp.clip(jax.random.uniform(splits[1], (TRIP,), jnp.float32, -0.95, 0.95), -0.95, 0.95)
    right_vecs = scatter_about(splits[2], (N, TRIP), 1.0, 6.0, ((0, 512),), jnp.float32)
    left_vecs = scatter_about(splits[3], (N, TRIP), 1.0, 6.0, ((0, 512),), jnp.float32)
    return dict(coefficients=coefficients, lambdas=lambdas, right_vecs=right_vecs, left_vecs=left_vecs)


epsilon = 1e-06

def chebyshev(lambdas, count):
    terms = [jnp.ones_like(lambdas), lambdas]
    while len(terms) < count:
        terms.append(2.0 * lambdas * terms[-1] - terms[-2])
    return jnp.stack(terms[:count])

def reference(coefficients, lambdas, right_vecs, left_vecs):
    weights = chebyshev(lambdas, K)
    right_sum = jnp.zeros((N, TRIP), jnp.float32)
    left_sum = jnp.zeros((N, TRIP), jnp.float32)
    for term in range(K):
        matrix = coefficients[term]
        right_sum = right_sum + jnp.dot(matrix, right_vecs * weights[term][None, :], precision=lax.Precision.HIGHEST, preferred_element_type=jnp.float32)
        left_sum = left_sum + lax.dot_general(matrix, left_vecs * weights[term][None, :], (((0,), (0,)), ((), ())), precision=lax.Precision.HIGHEST, preferred_element_type=jnp.float32)
    squares = jnp.stack([lax.optimization_barrier(jnp.mean(right_sum * right_sum, axis=0)), lax.optimization_barrier(jnp.mean(left_sum * left_sum, axis=0))])
    return (right_sum, left_sum, jnp.sqrt(squares + epsilon))
```

```python
import functools

import jax
import jax.numpy as jnp
from jax import lax
from jax.experimental import pallas as pl
from jax.experimental.pallas import tpu as pltpu
from jax.sharding import PartitionSpec as P

MESH = pl.DeviceIdType.MESH
N = 8192
K = 8
TRIP = 256
NX, NY, NZ = 4, 4, 16
EPSILON = 1e-06
F32 = jnp.float32
BF16 = jnp.bfloat16

ROW_OFFSETS = [(dx, dy, dc) for dx in (2, 1, 3, 0) for dy in (1, 0) for dc in (0, 1) if dx or dy or dc]
PLANE_OFFSETS = [(dx, dy, dc) for dx in (2, 1, 3, 0) for dy in (2, 1, 3, 0) for dc in (0, 1) if dx or dy or dc]
Z_OFFSETS = [8, 7, 9, 6, 10, 5, 11, 4, 12, 3, 13, 2, 14, 1, 15]


def split(value):
    high = value.astype(BF16)
    low = (value - high.astype(F32)).astype(BF16)
    return high, low


def dot(a, b):
    return jnp.dot(a, b, preferred_element_type=F32)


def kernel(
    a_hbm, lam_hbm, x_hbm, y_hbm, right_hbm, left_hbm, mean_ref,
    a_buf, a_hi, a_lo, lam_buf, w_row, w_col, x_buf, y_buf, y_t, r_acc, l_acc, l_out,
    relay_in, relay_out, raw_in, half_in, l_in, fin_r, fin_l, plane_buf, z_buf,
    a_sem, loc_sem, send_sem, x_sem, y_sem, yr_sem, yd_sem, rr_sem, raw_sem, half_sem, l_sem, p_sem, z_sem,
):
    row, col = lax.axis_index("row"), lax.axis_index("col")
    y_lo, x, core = row // 8, (row // 2) % 4, row % 2
    z, y_hi = col // 2, col % 2

    def row_at(off):
        dx, dy, dc = off
        return ((y_lo + dy) % 2) * 8 + ((x + dx) % 4) * 2 + (core + dc) % 2

    def row_dev(off):
        return (row_at(off), col)

    def plane_dev(off):
        dx, dy, dc = off
        yy = (y_hi * 2 + y_lo + dy) % 4
        return ((yy % 2) * 8 + ((x + dx) % 4) * 2 + (core + dc) % 2, z * 2 + yy // 2)

    def z_dev(dz):
        return (row, ((z + dz + 16) % 16) * 2 + y_hi)

    y_dev = (row, z * 2 + (1 - y_hi))

    def remote(src, dst, ssem, rsem, dev):
        return pltpu.make_async_remote_copy(
            src_ref=src, dst_ref=dst, send_sem=ssem, recv_sem=rsem, device_id=dev, device_id_type=MESH
        )

    for j in range(NZ):
        rows = pl.multiple_of(((z + j) % 16) * 32, 32)
        pltpu.make_async_copy(
            a_hbm.at[:, pl.ds(rows, 32), :], a_buf.at[:, pl.ds(j * 32, 32), :], a_sem.at[j]
        ).start()
    my_x = pl.multiple_of(row * 16, 16)
    mine, other = pl.multiple_of(y_hi * 16, 16), pl.multiple_of((1 - y_hi) * 16, 16)
    local = [
        pltpu.make_async_copy(lam_hbm, lam_buf, loc_sem.at[0]),
        pltpu.make_async_copy(x_hbm, x_buf.at[pl.ds(my_x, 16), :], loc_sem.at[1]),
        pltpu.make_async_copy(y_hbm, y_buf.at[0, pl.ds(mine, 16), :], loc_sem.at[2]),
    ]
    for copy in local:
        copy.start()

    barrier = pltpu.get_barrier_semaphore()
    partners = [row_dev(off) for off in ROW_OFFSETS] + [z_dev(1), z_dev(-1), z_dev(2), z_dev(-2), y_dev]
    for dev in partners:
        pl.semaphore_signal(barrier, inc=1, device_id=dev, device_id_type=MESH)
    pl.semaphore_wait(barrier, len(partners))

    def y_slot(rel, chunk):
        return y_buf.at[rel % 16, pl.ds(mine if chunk == 0 else other, 16), :]

    def y_forward(rel, chunk, up, src=None):
        src = y_slot(rel, chunk) if src is None else src
        step = abs(rel) // 2
        sign = 1 if up else -1
        if up or step < 3:
            remote(
                src, y_slot(rel - 2 * sign, chunk), send_sem.at[1], yr_sem.at[chunk, 0 if up else 1, step], z_dev(2 * sign)
            ).start()
        remote(src, y_slot(rel - sign, chunk), send_sem.at[1], yd_sem.at[chunk, 0 if up else 1, step], z_dev(sign)).start()

    def y_wait_relay(rel, chunk, up):
        sem = yr_sem.at[chunk, 0 if up else 1, abs(rel) // 2 - 1]
        remote(y_slot(rel, chunk), y_slot(rel, chunk), send_sem.at[1], sem, y_dev).wait_recv()

    def y_service(step, chunk):
        for up in (True, False):
            rel = -2 * step if up else 2 * step
            y_wait_relay(rel, chunk, up)
            y_forward(rel, chunk, up)

    for up in (True, False):
        y_forward(0, 0, up, src=y_hbm)
    remote(y_hbm, y_slot(0, 0), send_sem.at[1], y_sem, y_dev).start()
    for off in ROW_OFFSETS:
        remote(x_hbm, x_buf.at[pl.ds(my_x, 16), :], send_sem.at[0], x_sem, row_dev(off)).start()

    local[0].wait()
    lam = lam_buf[...]
    terms = [jnp.ones_like(lam), lam]
    while len(terms) < K:
        terms.append(2.0 * lam * terms[-1] - terms[-2])
    for k in range(K):
        w_row[k] = terms[k]
    lam_col = jnp.transpose(jnp.broadcast_to(lam, (128, TRIP)))
    w_col[0] = jnp.ones_like(lam_col)
    w_col[1] = lam_col
    for k in range(2, K):
        w_col[k] = 2.0 * lam_col * w_col[k - 1] - w_col[k - 2]

    def convert(j):
        rows = pl.ds(pl.multiple_of(j * 32, 32), 32)
        pltpu.make_async_copy(a_hbm.at[:, pl.ds(0, 32), :], a_buf.at[:, rows, :], a_sem.at[j]).wait()
        for k in range(K):
            a_hi[k, rows, :], a_lo[k, rows, :] = split(a_buf[k, rows, :])

    def convert_some(start, stop):
        @pl.loop(start, stop)
        def _(j):
            convert(j)

    def y_partner():
        remote(y_slot(0, 1), y_slot(0, 1), send_sem.at[1], y_sem, y_dev).wait_recv()
        for up in (True, False):
            y_forward(0, 1, up)

    convert_some(0, 8)
    y_partner()
    convert_some(8, 16)
    y_service(1, 0)

    local[1].wait()
    remote(x_buf.at[pl.ds(0, 240), :], x_buf.at[pl.ds(0, 240), :], send_sem.at[0], x_sem, y_dev).wait_recv()

    def right_term(k, first):
        xh, xl = split(x_buf[...] * w_row[k])
        ah, al = a_hi[k], a_lo[k]
        part = dot(ah, xh) + dot(al, xh) + dot(ah, xl)
        if first:
            r_acc[...] = part
        else:
            r_acc[...] += part

    def right_some(start, stop):
        @pl.loop(start, stop)
        def _(k):
            right_term(k, False)

    right_term(0, True)
    y_service(1, 1)
    right_some(1, 3)
    y_service(2, 0)
    right_some(3, 8)

    def r_rows(rel, half=None):
        if half is None:
            return pl.ds((rel % 16) * 32, 32)
        return pl.ds((rel % 16) * 32 + half * 16, 16)

    def relay(rel, half, up, src):
        i = (8 - rel) // 2 if up else (rel + 6) // 2
        d = 0 if up else 1
        return remote(
            src, relay_in.at[d, i, pl.ds(half * 16, 16), :], send_sem.at[2], rr_sem.at[d, i, half], z_dev(2 if up else -2)
        )

    for half in (0, 1):
        relay(8, half, True, r_acc.at[r_rows(8, half), :]).start()
    for i in range(4):
        for up in (True, False):
            rel, d = (7 - 2 * i, 0) if up else (2 * i - 7, 1)
            remote(
                r_acc.at[r_rows(rel), :], raw_in.at[d, i], send_sem.at[3], raw_sem.at[d, i], z_dev(1 if up else -1)
            ).start()

    def raw_wait(i, d):
        remote(raw_in.at[d, i], raw_in.at[d, i], send_sem.at[3], raw_sem.at[d, i], y_dev).wait_recv()

    def relay_wait(d, i, half):
        ref = relay_in.at[d, i, pl.ds(half * 16, 16), :]
        remote(ref, ref, send_sem.at[2], rr_sem.at[d, i, half], y_dev).wait_recv()

    def r_service(step):
        for d, up in ((1, False), (0, True)):
            raw_wait(step, d)
            rel = 6 - 2 * step if up else 2 * step - 6
            for half in (0, 1):
                hs = pl.ds(half * 16, 16)
                total = r_acc[r_rows(rel, half), :] + raw_in[d, step, hs, :]
                if up or step > 0:
                    i = step if up else step - 1
                    relay_wait(d, i, half)
                    total = total + relay_in[d, i, hs, :]
                relay_out[d, step, hs, :] = total
                relay(rel, half, up, relay_out.at[d, step, hs, :]).start()

    y_service(2, 1)
    y_service(3, 0)
    r_service(0)
    def y_service3(chunk):
        for up in (True, False):
            rel = -6 if up else 6
            y_wait_relay(rel, chunk, up)
            y_forward(rel, chunk, up)

    y_service3(1)

    def y_finish():
        for chunk in (0, 1):
            y_wait_relay(-8, chunk, True)
            for d in (0, 1):
                for step in range(4):
                    rel = -(2 * step + 1) if d == 0 else 2 * step + 1
                    remote(y_slot(rel, chunk), y_slot(rel, chunk), send_sem.at[1], yd_sem.at[chunk, d, step], y_dev).wait_recv()
        local[2].wait()

    y_finish()
    for j in range(4):
        y_t[:, j * 128 : (j + 1) * 128] = jnp.transpose(
            jnp.concatenate([y_buf[4 * j + i] for i in range(4)], axis=0)
        )

    def left_term(k, first):
        w = w_col[k]
        yh, yl = split(y_t[...] * jnp.concatenate([w] * 4, axis=1))
        ah, al = a_hi[k], a_lo[k]
        part = dot(yh, ah) + dot(yl, ah) + dot(yh, al)
        if first:
            l_acc[...] = part
        else:
            l_acc[...] += part

    def left_some(start, stop):
        @pl.loop(start, stop)
        def _(k):
            left_term(k, False)

    left_term(0, True)
    r_service(1)
    left_some(1, 8)
    l_out[...] = jnp.transpose(l_acc[...])
    for j, off in enumerate(ROW_OFFSETS):
        there = pl.multiple_of(row_at(off) * 16, 16)
        remote(l_out.at[pl.ds(there, 16), :], l_in.at[j], send_sem.at[4], l_sem, row_dev(off)).start()

    r_service(2)
    raw_wait(3, 0)
    raw_wait(3, 1)
    total = r_acc[r_rows(0), :] + raw_in[0, 3] + raw_in[1, 3]
    for half in (0, 1):
        relay_wait(0, 3, half)
        relay_wait(1, 2, half)
    fin_r[...] = total + relay_in[0, 3] + relay_in[1, 2]
    remote(fin_r.at[pl.ds(other, 16), :], half_in, send_sem.at[5], half_sem, y_dev).start()

    remote(l_in, l_in, send_sem.at[4], l_sem, y_dev).wait_recv()
    left = l_out[pl.ds(pl.multiple_of(row * 16, 16), 16), :]
    for j in range(len(ROW_OFFSETS)):
        left = left + l_in[j]
    fin_l[...] = left
    out_l = pltpu.make_async_copy(fin_l, left_hbm, loc_sem.at[3])
    out_l.start()
    remote(half_in, half_in, send_sem.at[5], half_sem, y_dev).wait_recv()
    right = fin_r[pl.ds(mine, 16), :] + half_in[...]
    half_in[...] = right
    out_r = pltpu.make_async_copy(half_in, right_hbm, loc_sem.at[4])
    out_r.start()

    squares = jnp.concatenate(
        [jnp.sum(right * right, axis=0, keepdims=True), jnp.sum(left * left, axis=0, keepdims=True)], axis=0
    )
    plane_buf[0] = squares
    for j, off in enumerate(PLANE_OFFSETS):
        remote(plane_buf.at[0], plane_buf.at[j + 1], send_sem.at[6], p_sem, plane_dev(off)).start()
    n = len(PLANE_OFFSETS)
    remote(plane_buf.at[pl.ds(1, n)], plane_buf.at[pl.ds(1, n)], send_sem.at[6], p_sem, y_dev).wait_recv()
    z_buf[0] = jnp.sum(plane_buf[...], axis=0)
    for j, dz in enumerate(Z_OFFSETS):
        remote(z_buf.at[0], z_buf.at[j + 1], send_sem.at[7], z_sem, z_dev(dz)).start()

    def sent(index, rows):
        remote(a_buf.at[0, pl.ds(0, rows), :], a_buf.at[0, pl.ds(0, rows), :], send_sem.at[index], x_sem, y_dev).wait_send()

    sent(0, 240)
    sent(1, 31 * 16)
    sent(2, 14 * 16)
    sent(3, 8 * 32)
    sent(4, 240)
    sent(5, 16)
    remote(plane_buf.at[pl.ds(1, n)], plane_buf.at[pl.ds(1, n)], send_sem.at[6], p_sem, y_dev).wait_send()
    out_l.wait()
    out_r.wait()
    m = len(Z_OFFSETS)
    last = remote(z_buf.at[pl.ds(1, m)], z_buf.at[pl.ds(1, m)], send_sem.at[7], z_sem, y_dev)
    last.wait_send()
    last.wait_recv()
    mean_ref[...] = jnp.sqrt(jnp.sum(z_buf[...], axis=0) / N + EPSILON)


def body(coefficients, lambdas, right_vecs, left_vecs):
    any_spec = pl.BlockSpec(memory_space=pl.ANY)
    vmem = pltpu.VMEM
    dma = pltpu.SemaphoreType.DMA
    return pl.pallas_call(
        kernel,
        out_shape=(
            jax.ShapeDtypeStruct((16, TRIP), F32),
            jax.ShapeDtypeStruct((16, TRIP), F32),
            jax.ShapeDtypeStruct((2, TRIP), F32),
        ),
        in_specs=[any_spec] * 4,
        out_specs=(any_spec, any_spec, pl.BlockSpec(memory_space=pltpu.VMEM)),
        scratch_shapes=[
            vmem((K, 512, 256), F32),
            vmem((K, 512, 256), BF16),
            vmem((K, 512, 256), BF16),
            vmem((1, TRIP), F32),
            vmem((K, 1, TRIP), F32),
            vmem((K, TRIP, 128), F32),
            vmem((256, TRIP), F32),
            vmem((NZ, 32, TRIP), F32),
            vmem((TRIP, 512), F32),
            vmem((512, TRIP), F32),
            vmem((TRIP, 256), F32),
            vmem((256, TRIP), F32),
            vmem((2, 4, 32, TRIP), F32),
            vmem((2, 3, 32, TRIP), F32),
            vmem((2, 4, 32, TRIP), F32),
            vmem((16, TRIP), F32),
            vmem((15, 16, TRIP), F32),
            vmem((32, TRIP), F32),
            vmem((16, TRIP), F32),
            vmem((32, 2, TRIP), F32),
            vmem((16, 2, TRIP), F32),
            dma((16,)),
            dma((5,)),
            dma((8,)),
            dma,
            dma,
            dma((2, 2, 4)),
            dma((2, 2, 4)),
            dma((2, 4, 2)),
            dma((2, 4)),
            dma,
            dma,
            dma,
            dma,
        ],
        compiler_params=pltpu.CompilerParams(
            collective_id=0, has_side_effects=True, vmem_limit_bytes=56 * 1024 * 1024
        ),
    )(coefficients, lambdas.reshape(1, TRIP), right_vecs, left_vecs)


def solution(mesh):
    return jax.shard_map(
        body,
        mesh=mesh,
        in_specs=(P(None, "row", "col"), P(), P(("col", "row"), None), P(("row", "col"), None)),
        out_specs=(P(("row", "col"), None), P(("col", "row"), None), P()),
        check_vma=False,
    )
```

```python
import functools

import jax
import jax.numpy as jnp
from jax import lax
from jax.experimental import pallas as pl
from jax.experimental.pallas import tpu as pltpu
from jax.sharding import PartitionSpec as P

MESH = pl.DeviceIdType.MESH
N = 8192
K = 8
TRIP = 256
NX, NY, NZ = 4, 4, 16
EPSILON = 1e-06
F32 = jnp.float32
BF16 = jnp.bfloat16

ROW_OFFSETS = [(dx, dy, dc) for dx in (2, 1, 3, 0) for dy in (1, 0) for dc in (0, 1) if dx or dy or dc]
PLANE_OFFSETS = [(dx, dy, dc) for dx in (2, 1, 3, 0) for dy in (2, 1, 3, 0) for dc in (0, 1) if dx or dy or dc]
Z_OFFSETS = [8, 7, 9, 6, 10, 5, 11, 4, 12, 3, 13, 2, 14, 1, 15]


def split(value):
    high = value.astype(BF16)
    low = (value - high.astype(F32)).astype(BF16)
    return high, low


def dot(a, b):
    return jnp.dot(a, b, preferred_element_type=F32)


def slot(rel):
    return (rel + 4) % 16


def kernel(
    a_hbm, lam_hbm, x_hbm, y_hbm, right_ref, left_ref, mean_ref,
    a_buf, a_split, lam_buf, w_row, w_col, x_buf, y_buf, y_t, r_acc, l_acc, l_out,
    relay_in, relay_out, raw_in, last_in, base, half_in, l_in, plane_buf, z_buf,
    a_sem, loc_sem, send_sem, x_sem, y_sem, yr_sem, yd_sem, rr_sem, raw_sem, half_sem, l_sem, p_sem, z_sem,
):
    row, col = lax.axis_index("row"), lax.axis_index("col")
    y_lo, x, core = row // 8, (row // 2) % 4, row % 2
    z, y_hi = col // 2, col % 2

    def row_at(off):
        dx, dy, dc = off
        return ((y_lo + dy) % 2) * 8 + ((x + dx) % 4) * 2 + (core + dc) % 2

    def row_dev(off):
        return (row_at(off), col)

    def plane_dev(off):
        dx, dy, dc = off
        yy = (y_hi * 2 + y_lo + dy) % 4
        return ((yy % 2) * 8 + ((x + dx) % 4) * 2 + (core + dc) % 2, z * 2 + yy // 2)

    def z_dev(dz):
        return (row, ((z + dz + 16) % 16) * 2 + y_hi)

    y_dev = (row, z * 2 + (1 - y_hi))

    def remote(src, dst, ssem, rsem, dev):
        return pltpu.make_async_remote_copy(
            src_ref=src, dst_ref=dst, send_sem=ssem, recv_sem=rsem, device_id=dev, device_id_type=MESH
        )

    def other_dev(dz):
        return (row, ((z + dz + 16) % 16) * 2 + (1 - y_hi))

    barrier = pltpu.get_barrier_semaphore()
    partners = [row_dev(off) for off in ROW_OFFSETS] + [z_dev(1), z_dev(-1), z_dev(2), z_dev(-2)]
    partners += [y_dev, other_dev(1), other_dev(-1)]
    for dev in partners:
        pl.semaphore_signal(barrier, inc=1, device_id=dev, device_id_type=MESH)

    my_x = pl.multiple_of(row * 16, 16)
    mine, other = pl.multiple_of(y_hi * 16, 16), pl.multiple_of((1 - y_hi) * 16, 16)
    local = [
        pltpu.make_async_copy(lam_hbm, lam_buf, loc_sem.at[0]),
        pltpu.make_async_copy(x_hbm, x_buf.at[pl.ds(my_x, 16), :], loc_sem.at[1]),
        pltpu.make_async_copy(y_hbm, y_buf.at[slot(0), pl.ds(mine, 16), :], loc_sem.at[2]),
    ]
    for copy in local:
        copy.start()
    for j in range(NZ):
        rows = pl.multiple_of(((z + j - 4 + 16) % 16) * 32, 32)
        pltpu.make_async_copy(
            a_hbm.at[:, pl.ds(rows, 32), :], a_buf.at[:, pl.ds(j * 32, 32), :], a_sem.at[j]
        ).start()
    pl.semaphore_wait(barrier, len(partners))

    def y_slot(rel, chunk=0):
        return y_buf.at[slot(rel), pl.ds(mine if chunk == 0 else other, 16), :]

    def y_send(rel, to, sem, dev):
        src = y_hbm if rel == 0 else y_slot(rel)
        remote(src, y_slot(to), send_sem.at[1], sem, dev).start()

    def y_wait(rel, chunk, sem):
        ref = y_slot(rel, chunk)
        remote(ref, ref, send_sem.at[1], sem, y_dev).wait_recv()

    def y_relays(step):
        for d, sign in ((0, 1), (1, -1)):
            rel = -2 * step * sign
            if sign > 0 or step < 3:
                y_send(rel, rel - 2 * sign, yr_sem.at[0, d, step], z_dev(2 * sign))
            if sign > 0 and step == 3:
                y_send(rel, rel - 2 * sign, yr_sem.at[1, 0, 0], other_dev(2 * sign))

    def y_drops(step):
        for d, sign in ((0, 1), (1, -1)):
            rel = -2 * step * sign
            y_send(rel, rel - sign, yd_sem.at[0, d, step], z_dev(sign))

    def y_copies(step):
        for d, sign in ((0, 1), (1, -1)):
            rel = -2 * step * sign
            if step > 0:
                y_send(rel, rel, yr_sem.at[1, d, step], y_dev)
            elif sign > 0:
                y_send(rel, rel, y_sem, y_dev)
        for d, sign in ((0, 1), (1, -1)):
            rel = -2 * step * sign
            y_send(rel, rel - sign, yd_sem.at[1, d, step], other_dev(sign))

    def y_service(step):
        if step == 3:
            y_wait_copy(1)
        for d, sign in ((0, 1), (1, -1)):
            y_wait(-2 * step * sign, 0, yr_sem.at[0, d, step - 1])
        y_relays(step)
        y_drops(step)
        if step > 1:
            y_copies(step)

    def y_wait_copy(step):
        for d, sign in ((0, 1), (1, -1)):
            y_wait(-2 * step * sign, 1, yr_sem.at[1, d, step])

    def y_wait_drop(step):
        for chunk in (0, 1):
            for d, sign in ((0, -1), (1, 1)):
                y_wait(sign * (2 * step + 1), chunk, yd_sem.at[chunk, d, step])

    y_relays(0)
    for off in ROW_OFFSETS:
        remote(x_hbm, x_buf.at[pl.ds(my_x, 16), :], send_sem.at[0], x_sem, row_dev(off)).start()
    y_drops(0)

    local[0].wait()
    lam = lam_buf[...]
    terms = [jnp.ones_like(lam), lam]
    while len(terms) < K:
        terms.append(2.0 * lam * terms[-1] - terms[-2])
    for k in range(K):
        w_row[k] = terms[k]
    lam_col = jnp.transpose(jnp.broadcast_to(lam, (128, TRIP)))
    w_col[0] = jnp.ones_like(lam_col)
    w_col[1] = lam_col
    for k in range(2, K):
        w_col[k] = 2.0 * lam_col * w_col[k - 1] - w_col[k - 2]

    @pl.loop(0, NZ)
    def _(j):
        rows = pl.ds(pl.multiple_of(j * 32, 32), 32)
        pltpu.make_async_copy(a_hbm.at[:, pl.ds(0, 32), :], a_buf.at[:, rows, :], a_sem.at[j]).wait()
        part, start = j // 8, pl.multiple_of((j % 8) * 32, 32)
        for k in range(K):
            high, low = split(a_buf[k, rows, :])
            a_split[k, part, pl.ds(start, 32), :] = high
            a_split[k, part, pl.ds(start + 256, 32), :] = low

    y_service(1)
    local[1].wait()
    remote(x_buf.at[pl.ds(0, 240), :], x_buf.at[pl.ds(0, 240), :], send_sem.at[0], x_sem, y_dev).wait_recv()

    def right_half(part):
        rows = pl.ds(part * 256, 256)

        def term(k):
            xh, xl = split(x_buf[...] * w_row[k])
            both = dot(a_split[k, part], xh)
            return both[:256] + both[256:] + dot(a_split[k, part, :256, :], xl)

        r_acc[rows, :] = term(0)
        for k in range(1, K):
            r_acc[rows, :] += term(k)

    def half_rows(half):
        return pl.ds(mine if half == 0 else other, 16)

    def r_block(rel, half):
        return pl.ds(slot(rel) * 32 + (mine if half == 0 else other), 16)

    def relay(rel, half, up, src):
        i, d = ((8 - rel) // 2 if up else (rel + 6) // 2), (0 if up else 1)
        last = abs(rel) == 2
        dst = last_in.at[d, half] if last else relay_in.at[d, i, half_rows(half), :]
        dz = 2 if up else -2
        return remote(src, dst, send_sem.at[2], rr_sem.at[d, i, half], other_dev(dz) if last and half == 1 else z_dev(dz))

    def raw(rel):
        up = rel > 0
        i, d = ((7 - rel) // 2 if up else (rel + 7) // 2), (0 if up else 1)
        rows = pl.ds(slot(rel) * 32, 32)
        return remote(r_acc.at[rows, :], raw_in.at[d, i], send_sem.at[3], raw_sem.at[d, i], z_dev(1 if up else -1))

    def raw_wait(i, d):
        remote(raw_in.at[d, i], raw_in.at[d, i], send_sem.at[3], raw_sem.at[d, i], y_dev).wait_recv()

    def r_service(step):
        for d, up in ((1, False), (0, True)):
            raw_wait(step, d)
        for half in (1, 0):
            for d, up in ((1, False), (0, True)):
                rel = 6 - 2 * step if up else 2 * step - 6
                hs = half_rows(half)
                total = r_acc[r_block(rel, half), :] + raw_in[d, step, hs, :]
                if up or step > 0:
                    i = step if up else step - 1
                    ref = relay_in.at[d, i, hs, :]
                    remote(ref, ref, send_sem.at[2], rr_sem.at[d, i, half], y_dev).wait_recv()
                    total = total + relay_in[d, i, hs, :]
                relay_out[d, step, hs, :] = total
                relay(rel, half, up, relay_out.at[d, step, hs, :]).start()

    right_half(1)
    for half in (1, 0):
        relay(8, half, True, r_acc.at[r_block(8, half), :]).start()
    for rel in (-7, 7):
        raw(rel).start()
    y_copies(0)
    y_copies(1)
    right_half(0)

    y_service(2)
    r_service(0)
    for rel in (-5, 5):
        raw(rel).start()
    y_service(3)

    def turn(part):
        for i in (0, 1):
            y_t[part, :, i * 128 : (i + 1) * 128] = jnp.transpose(
                jnp.concatenate([y_buf[8 * part + 4 * i + j] for j in range(4)], axis=0)
            )

    def left_half(part):
        def term(k):
            w = w_col[k]
            yh, yl = split(y_t[part] * jnp.concatenate([w, w], axis=1))
            both = dot(jnp.concatenate([yh, yl], axis=0), a_split[k, part, :256, :])
            return both[:256] + both[256:] + dot(yh, a_split[k, part, 256:, :])

        for k in range(K):
            if part == 0 and k == 0:
                l_acc[...] = term(k)
            else:
                l_acc[...] += term(k)

    local[2].wait()
    y_wait(0, 1, y_sem)
    y_wait_copy(2)
    y_wait_drop(0)
    y_wait_drop(1)
    turn(0)
    left_half(0)
    r_service(1)
    for rel in (-3, 3, -1, 1):
        raw(rel).start()
    y_wait(-8, 0, yr_sem.at[0, 0, 3])
    y_wait(-8, 1, yr_sem.at[1, 0, 0])
    y_wait_copy(3)
    y_wait_drop(2)
    y_wait_drop(3)
    turn(1)
    left_half(1)
    l_out[...] = jnp.transpose(l_acc[...])
    for j, off in enumerate(ROW_OFFSETS):
        there = pl.multiple_of(row_at(off) * 16, 16)
        remote(l_out.at[pl.ds(there, 16), :], l_in.at[j], send_sem.at[4], l_sem, row_dev(off)).start()
    raw_wait(3, 0)
    raw_wait(3, 1)
    base[...] = r_acc[pl.ds(slot(0) * 32, 32), :] + raw_in[0, 3] + raw_in[1, 3]
    remote(base.at[pl.ds(other, 16), :], half_in, send_sem.at[5], half_sem, y_dev).start()
    r_service(2)

    remote(l_in, l_in, send_sem.at[4], l_sem, y_dev).wait_recv()
    left = l_out[pl.ds(pl.multiple_of(row * 16, 16), 16), :]
    for j in range(len(ROW_OFFSETS)):
        left = left + l_in[j]
    left_ref[...] = left
    remote(half_in, half_in, send_sem.at[5], half_sem, y_dev).wait_recv()
    right = base[pl.ds(mine, 16), :] + half_in[...]
    for d, i in ((0, 3), (1, 2)):
        for half in (0, 1):
            ref = last_in.at[d, half]
            remote(ref, ref, send_sem.at[2], rr_sem.at[d, i, half], y_dev).wait_recv()
            right = right + last_in[d, half]
    right_ref[...] = right

    squares = jnp.concatenate(
        [jnp.sum(right * right, axis=0, keepdims=True), jnp.sum(left * left, axis=0, keepdims=True)], axis=0
    )
    plane_buf[0] = squares
    for j, off in enumerate(PLANE_OFFSETS):
        remote(plane_buf.at[0], plane_buf.at[j + 1], send_sem.at[6], p_sem, plane_dev(off)).start()
    n = len(PLANE_OFFSETS)
    remote(plane_buf.at[pl.ds(1, n)], plane_buf.at[pl.ds(1, n)], send_sem.at[6], p_sem, y_dev).wait_recv()
    z_buf[0] = jnp.sum(plane_buf[...], axis=0)
    for j, dz in enumerate(Z_OFFSETS):
        remote(z_buf.at[0], z_buf.at[j + 1], send_sem.at[7], z_sem, z_dev(dz)).start()

    def sent(index, rows):
        remote(a_buf.at[0, pl.ds(0, rows), :], a_buf.at[0, pl.ds(0, rows), :], send_sem.at[index], x_sem, y_dev).wait_send()

    sent(0, 240)
    sent(1, 31 * 16)
    sent(2, 14 * 16)
    sent(3, 8 * 32)
    sent(4, 240)
    sent(5, 16)
    remote(plane_buf.at[pl.ds(1, n)], plane_buf.at[pl.ds(1, n)], send_sem.at[6], p_sem, y_dev).wait_send()
    m = len(Z_OFFSETS)
    last = remote(z_buf.at[pl.ds(1, m)], z_buf.at[pl.ds(1, m)], send_sem.at[7], z_sem, y_dev)
    last.wait_send()
    last.wait_recv()
    mean_ref[...] = jnp.sqrt(jnp.sum(z_buf[...], axis=0) / N + EPSILON)


def finish(right_ref, left_ref, mean_ref, right_out, left_out, mean_out, sem):
    copies = [
        pltpu.make_async_copy(right_ref, right_out, sem.at[0]),
        pltpu.make_async_copy(left_ref, left_out, sem.at[1]),
        pltpu.make_async_copy(mean_ref, mean_out, sem.at[2]),
    ]
    for copy in copies:
        copy.start()
    for copy in copies:
        copy.wait()


def body(coefficients, lambdas, right_vecs, left_vecs):
    any_spec = pl.BlockSpec(memory_space=pl.ANY)
    vmem = pltpu.VMEM
    dma = pltpu.SemaphoreType.DMA
    shapes = ((16, TRIP), (16, TRIP), (2, TRIP))
    vmem_spec = pl.BlockSpec(memory_space=vmem)
    results = pl.pallas_call(
        kernel,
        out_shape=tuple(vmem(shape, F32) for shape in shapes),
        in_specs=[any_spec] * 4,
        out_specs=(vmem_spec,) * 3,
        scratch_shapes=[
            vmem((K, 512, 256), F32),
            vmem((K, 2, 512, 256), BF16),
            vmem((1, TRIP), F32),
            vmem((K, 1, TRIP), F32),
            vmem((K, TRIP, 128), F32),
            vmem((256, TRIP), F32),
            vmem((NZ, 32, TRIP), F32),
            vmem((2, TRIP, 256), F32),
            vmem((512, TRIP), F32),
            vmem((TRIP, 256), F32),
            vmem((256, TRIP), F32),
            vmem((2, 3, 32, TRIP), F32),
            vmem((2, 3, 32, TRIP), F32),
            vmem((2, 4, 32, TRIP), F32),
            vmem((2, 2, 16, TRIP), F32),
            vmem((32, TRIP), F32),
            vmem((16, TRIP), F32),
            vmem((15, 16, TRIP), F32),
            vmem((32, 2, TRIP), F32),
            vmem((16, 2, TRIP), F32),
            dma((16,)),
            dma((3,)),
            dma((8,)),
            dma,
            dma,
            dma((2, 2, 4)),
            dma((2, 2, 4)),
            dma((2, 4, 2)),
            dma((2, 4)),
            dma,
            dma,
            dma,
            dma,
        ],
        compiler_params=pltpu.CompilerParams(
            collective_id=0, has_side_effects=True, vmem_limit_bytes=56 * 1024 * 1024
        ),
    )(coefficients, lambdas.reshape(1, TRIP), right_vecs, left_vecs)
    return pl.pallas_call(
        finish,
        out_shape=tuple(jax.ShapeDtypeStruct(shape, F32) for shape in shapes),
        in_specs=[vmem_spec] * 3,
        out_specs=(any_spec,) * 3,
        scratch_shapes=[dma((3,))],
    )(*[pltpu.with_memory_space_constraint(result, vmem) for result in results])


def solution(mesh):
    return jax.shard_map(
        body,
        mesh=mesh,
        in_specs=(P(None, "row", "col"), P(), P(("col", "row"), None), P(("row", "col"), None)),
        out_specs=(P(("row", "col"), None), P(("col", "row"), None), P()),
        check_vma=False,
    )
```

```python
import functools

import jax
import jax.numpy as jnp
from jax import lax
from jax.experimental import pallas as pl
from jax.experimental.pallas import tpu as pltpu
from jax.sharding import PartitionSpec as P

MESH = pl.DeviceIdType.MESH
N = 8192
K = 8
TRIP = 256
NX, NY, NZ = 4, 4, 16
EPSILON = 1e-06
F32 = jnp.float32
BF16 = jnp.bfloat16

ROW_OFFSETS = [(dx, dy, dc) for dx in (2, 1, 3, 0) for dy in (1, 0) for dc in (0, 1) if dx or dy or dc]
NEAR = [4, -4, 3, -3, 2, -2, 1, -1]
FAR = [(8, 4), (7, 3), (-7, -3), (6, 2), (-6, -2), (5, 1), (-5, -1)]
PLANE_OFFSETS = [(dx, dy, dc) for dx in (2, 1, 3, 0) for dy in (2, 1, 3, 0) for dc in (0, 1) if dx or dy or dc]
Z_OFFSETS = [8, 7, 9, 6, 10, 5, 11, 4, 12, 3, 13, 2, 14, 1, 15]


def split(value):
    high = value.astype(BF16)
    low = (value - high.astype(F32)).astype(BF16)
    return high, low


def dot(a, b):
    return jnp.dot(a, b, preferred_element_type=F32)


def slot(rel):
    return (rel + 4) % 16


def kernel(
    a_hbm, lam_hbm, x_hbm, y_hbm, right_ref, left_ref, mean_ref,
    a_buf, a_split, lam_buf, w_row, w_col, x_buf, y_buf, y_t, r_acc, l_acc, l_out,
    mid_in, mid_out, fin_in, fin_out, cross_in, l_in, plane_buf, z_buf,
    a_sem, loc_sem, send_sem, x_sem, y_sem, mid_sem, fin_sem, cross_sem, l_sem, p_sem, z_sem,
):
    row, col = lax.axis_index("row"), lax.axis_index("col")
    y_lo, x, core = row // 8, (row // 2) % 4, row % 2
    z, y_hi = col // 2, col % 2

    def row_at(off):
        dx, dy, dc = off
        return ((y_lo + dy) % 2) * 8 + ((x + dx) % 4) * 2 + (core + dc) % 2

    def row_dev(off):
        return (row_at(off), col)

    def plane_dev(off):
        dx, dy, dc = off
        yy = (y_hi * 2 + y_lo + dy) % 4
        return ((yy % 2) * 8 + ((x + dx) % 4) * 2 + (core + dc) % 2, z * 2 + yy // 2)

    def z_dev(dz):
        return (row, ((z + dz + 16) % 16) * 2 + y_hi)

    y_dev = (row, z * 2 + (1 - y_hi))

    def remote(src, dst, ssem, rsem, dev):
        return pltpu.make_async_remote_copy(
            src_ref=src, dst_ref=dst, send_sem=ssem, recv_sem=rsem, device_id=dev, device_id_type=MESH
        )

    def other_dev(dz):
        return (row, ((z + dz + 16) % 16) * 2 + (1 - y_hi))

    barrier = pltpu.get_barrier_semaphore()
    partners = [row_dev(off) for off in ROW_OFFSETS] + [z_dev(dz) for dz in NEAR] + [y_dev]
    for dev in partners:
        pl.semaphore_signal(barrier, inc=1, device_id=dev, device_id_type=MESH)

    my_x = pl.multiple_of(row * 16, 16)
    mine, other = pl.multiple_of(y_hi * 16, 16), pl.multiple_of((1 - y_hi) * 16, 16)
    local = [
        pltpu.make_async_copy(lam_hbm, lam_buf, loc_sem.at[0]),
        pltpu.make_async_copy(x_hbm, x_buf.at[pl.ds(my_x, 16), :], loc_sem.at[1]),
        pltpu.make_async_copy(y_hbm, y_buf.at[slot(0), pl.ds(mine, 16), :], loc_sem.at[2]),
    ]
    for copy in local:
        copy.start()
    for j in range(NZ):
        rows = pl.multiple_of(((z + j - 4 + 16) % 16) * 32, 32)
        pltpu.make_async_copy(
            a_hbm.at[:, pl.ds(rows, 32), :], a_buf.at[:, pl.ds(j * 32, 32), :], a_sem.at[j]
        ).start()
    pl.semaphore_wait(barrier, len(partners))

    def y_slot(rel, chunk=0):
        return y_buf.at[slot(rel), pl.ds(mine if chunk == 0 else other, 16), :]

    def y_send(rel, to, chunk, dev):
        src = y_hbm if rel == 0 else y_slot(rel)
        remote(src, y_slot(to), send_sem.at[1], y_sem.at[chunk, slot(to)], dev).start()

    def y_wait(rel, chunk):
        ref = y_slot(rel, chunk)
        remote(ref, ref, send_sem.at[1], y_sem.at[chunk, slot(rel)], y_dev).wait_recv()

    for dz in NEAR[:2]:
        y_send(0, -dz, 0, z_dev(dz))
    for off in ROW_OFFSETS:
        remote(x_hbm, x_buf.at[pl.ds(my_x, 16), :], send_sem.at[0], x_sem, row_dev(off)).start()
    for dz in NEAR[2:]:
        y_send(0, -dz, 0, z_dev(dz))
    y_send(0, 0, 1, y_dev)

    local[0].wait()
    lam = lam_buf[...]
    terms = [jnp.ones_like(lam), lam]
    while len(terms) < K:
        terms.append(2.0 * lam * terms[-1] - terms[-2])
    for k in range(K):
        w_row[k] = terms[k]
    lam_col = jnp.transpose(jnp.broadcast_to(lam, (128, TRIP)))
    w_col[0] = jnp.ones_like(lam_col)
    w_col[1] = lam_col
    for k in range(2, K):
        w_col[k] = 2.0 * lam_col * w_col[k - 1] - w_col[k - 2]

    @pl.loop(0, NZ)
    def _(j):
        rows = pl.ds(pl.multiple_of(j * 32, 32), 32)
        pltpu.make_async_copy(a_hbm.at[:, pl.ds(0, 32), :], a_buf.at[:, rows, :], a_sem.at[j]).wait()
        part, start = j // 8, pl.multiple_of((j % 8) * 32, 32)
        for k in range(K):
            high, low = split(a_buf[k, rows, :])
            a_split[k, part, pl.ds(start, 32), :] = high
            a_split[k, part, pl.ds(start + 256, 32), :] = low

    def y_far(chunk):
        for far, dz in FAR:
            y_send(-4 if dz > 0 else 4, -far, chunk, z_dev(dz) if chunk == 0 else other_dev(dz))

    def y_near():
        for dz in NEAR[2:]:
            y_wait(dz, 0)
        for dz in NEAR:
            y_send(dz, dz, 1, y_dev)

    y_wait(4, 0)
    y_wait(-4, 0)
    y_far(0)
    y_near()
    local[1].wait()
    remote(x_buf.at[pl.ds(0, 240), :], x_buf.at[pl.ds(0, 240), :], send_sem.at[0], x_sem, y_dev).wait_recv()

    def right_half(part):
        rows = pl.ds(part * 256, 256)

        def term(k):
            xh, xl = split(x_buf[...] * w_row[k])
            both = dot(a_split[k, part], xh)
            return both[:256] + both[256:] + dot(a_split[k, part, :256, :], xl)

        r_acc[rows, :] = term(0)
        for k in range(1, K):
            r_acc[rows, :] += term(k)

    def cross(rel):
        rows = pl.ds(slot(rel) * 32 + other, 16)
        n = slot(rel)
        return remote(r_acc.at[rows, :], cross_in.at[n], send_sem.at[5], cross_sem.at[n], y_dev)

    def pair(rel):
        ref = cross_in.at[slot(rel)]
        remote(ref, ref, send_sem.at[5], cross_sem.at[slot(rel)], y_dev).wait_recv()
        return r_acc[pl.ds(slot(rel) * 32 + mine, 16), :] + cross_in[slot(rel)]

    def r_far():
        for i, (far, dz) in enumerate(FAR):
            mid_out[i] = pair(far)
            remote(mid_out.at[i], mid_in.at[i], send_sem.at[2], mid_sem.at[i], z_dev(dz)).start()

    def r_send(i, value):
        fin_out[i] = value
        remote(fin_out.at[i], fin_in.at[i], send_sem.at[3], fin_sem.at[i], z_dev(NEAR[i])).start()

    def r_relay():
        for j, dz in enumerate(NEAR[:2]):
            total = pair(dz)
            for i, (_, hop) in enumerate(FAR):
                if hop * dz > 0:
                    remote(mid_in.at[i], mid_in.at[i], send_sem.at[2], mid_sem.at[i], y_dev).wait_recv()
                    total = total + mid_in[i]
            r_send(j, total)

    def r_near():
        for i, dz in enumerate(NEAR[2:]):
            r_send(i + 2, pair(dz))

    right_half(1)
    for rel in (8, 7, -7, 6, -6, 5, -5, 4):
        cross(rel).start()
    y_far(1)
    right_half(0)
    r_far()
    for rel in (-4, 3, -3, 2, -2, 1, -1, 0):
        cross(rel).start()

    def turn(part):
        for i in (0, 1):
            y_t[part, :, i * 128 : (i + 1) * 128] = jnp.transpose(
                jnp.concatenate([y_buf[8 * part + 4 * i + j] for j in range(4)], axis=0)
            )

    def left_half(part):
        def term(k):
            w = w_col[k]
            yh, yl = split(y_t[part] * jnp.concatenate([w, w], axis=1))
            both = dot(jnp.concatenate([yh, yl], axis=0), a_split[k, part, :256, :])
            return both[:256] + both[256:] + dot(yh, a_split[k, part, 256:, :])

        for k in range(K):
            if part == 0 and k == 0:
                l_acc[...] = term(k)
            else:
                l_acc[...] += term(k)

    local[2].wait()
    for rel in [0] + NEAR:
        if rel != 4:
            y_wait(rel, 1)
    turn(0)
    left_half(0)
    y_wait(4, 1)
    for far, _ in FAR:
        y_wait(-far, 0)
        y_wait(-far, 1)
    turn(1)
    left_half(1)
    l_out[...] = jnp.transpose(l_acc[...])
    for j, off in enumerate(ROW_OFFSETS):
        there = pl.multiple_of(row_at(off) * 16, 16)
        remote(l_out.at[pl.ds(there, 16), :], l_in.at[j], send_sem.at[4], l_sem, row_dev(off)).start()
    r_relay()
    r_near()
    right = pair(0)

    remote(l_in, l_in, send_sem.at[4], l_sem, y_dev).wait_recv()
    left = l_out[pl.ds(pl.multiple_of(row * 16, 16), 16), :]
    for j in range(len(ROW_OFFSETS)):
        left = left + l_in[j]
    left_ref[...] = left
    for i in range(2, 8):
        remote(fin_in.at[i], fin_in.at[i], send_sem.at[3], fin_sem.at[i], y_dev).wait_recv()
        right = right + fin_in[i]
    for i in (0, 1):
        remote(fin_in.at[i], fin_in.at[i], send_sem.at[3], fin_sem.at[i], y_dev).wait_recv()
        right = right + fin_in[i]
    right_ref[...] = right

    squares = jnp.concatenate(
        [jnp.sum(right * right, axis=0, keepdims=True), jnp.sum(left * left, axis=0, keepdims=True)], axis=0
    )
    plane_buf[0] = squares
    for j, off in enumerate(PLANE_OFFSETS):
        remote(plane_buf.at[0], plane_buf.at[j + 1], send_sem.at[6], p_sem, plane_dev(off)).start()
    n = len(PLANE_OFFSETS)
    remote(plane_buf.at[pl.ds(1, n)], plane_buf.at[pl.ds(1, n)], send_sem.at[6], p_sem, y_dev).wait_recv()
    z_buf[0] = jnp.sum(plane_buf[...], axis=0)
    for j, dz in enumerate(Z_OFFSETS):
        remote(z_buf.at[0], z_buf.at[j + 1], send_sem.at[7], z_sem, z_dev(dz)).start()

    def sent(index, rows):
        remote(a_buf.at[0, pl.ds(0, rows), :], a_buf.at[0, pl.ds(0, rows), :], send_sem.at[index], x_sem, y_dev).wait_send()

    sent(0, 240)
    sent(1, 31 * 16)
    sent(2, 7 * 16)
    sent(3, 8 * 16)
    sent(4, 240)
    sent(5, 256)
    remote(plane_buf.at[pl.ds(1, n)], plane_buf.at[pl.ds(1, n)], send_sem.at[6], p_sem, y_dev).wait_send()
    m = len(Z_OFFSETS)
    last = remote(z_buf.at[pl.ds(1, m)], z_buf.at[pl.ds(1, m)], send_sem.at[7], z_sem, y_dev)
    last.wait_send()
    last.wait_recv()
    mean_ref[...] = jnp.sqrt(jnp.sum(z_buf[...], axis=0) / N + EPSILON)


def finish(right_ref, left_ref, mean_ref, right_out, left_out, mean_out, sem):
    copies = [
        pltpu.make_async_copy(right_ref, right_out, sem.at[0]),
        pltpu.make_async_copy(left_ref, left_out, sem.at[1]),
        pltpu.make_async_copy(mean_ref, mean_out, sem.at[2]),
    ]
    for copy in copies:
        copy.start()
    for copy in copies:
        copy.wait()


def body(coefficients, lambdas, right_vecs, left_vecs):
    any_spec = pl.BlockSpec(memory_space=pl.ANY)
    vmem = pltpu.VMEM
    dma = pltpu.SemaphoreType.DMA
    shapes = ((16, TRIP), (16, TRIP), (2, TRIP))
    vmem_spec = pl.BlockSpec(memory_space=vmem)
    results = pl.pallas_call(
        kernel,
        out_shape=tuple(vmem(shape, F32) for shape in shapes),
        in_specs=[any_spec] * 4,
        out_specs=(vmem_spec,) * 3,
        scratch_shapes=[
            vmem((K, 512, 256), F32),
            vmem((K, 2, 512, 256), BF16),
            vmem((1, TRIP), F32),
            vmem((K, 1, TRIP), F32),
            vmem((K, TRIP, 128), F32),
            vmem((256, TRIP), F32),
            vmem((NZ, 32, TRIP), F32),
            vmem((2, TRIP, 256), F32),
            vmem((512, TRIP), F32),
            vmem((TRIP, 256), F32),
            vmem((256, TRIP), F32),
            vmem((7, 16, TRIP), F32),
            vmem((7, 16, TRIP), F32),
            vmem((8, 16, TRIP), F32),
            vmem((8, 16, TRIP), F32),
            vmem((NZ, 16, TRIP), F32),
            vmem((15, 16, TRIP), F32),
            vmem((32, 2, TRIP), F32),
            vmem((16, 2, TRIP), F32),
            dma((16,)),
            dma((3,)),
            dma((8,)),
            dma,
            dma((2, NZ)),
            dma((7,)),
            dma((8,)),
            dma((NZ,)),
            dma,
            dma,
            dma,
        ],
        compiler_params=pltpu.CompilerParams(
            collective_id=0, has_side_effects=True, vmem_limit_bytes=56 * 1024 * 1024
        ),
    )(coefficients, lambdas.reshape(1, TRIP), right_vecs, left_vecs)
    return pl.pallas_call(
        finish,
        out_shape=tuple(jax.ShapeDtypeStruct(shape, F32) for shape in shapes),
        in_specs=[vmem_spec] * 3,
        out_specs=(any_spec,) * 3,
        scratch_shapes=[dma((3,))],
    )(*[pltpu.with_memory_space_constraint(result, vmem) for result in results])


def solution(mesh):
    return jax.shard_map(
        body,
        mesh=mesh,
        in_specs=(P(None, "row", "col"), P(), P(("col", "row"), None), P(("row", "col"), None)),
        out_specs=(P(("row", "col"), None), P(("col", "row"), None), P()),
        check_vma=False,
    )
```
